32 devices in a mesh: space: 16 (over z, y, core), grp: 2 (over x).
Axes of the slice: x: 2, y: 2, z: 4, core: 2. Of those that a mesh axis runs over, the one named last changes fastest.
Arguments:
- diag_blocks: float32 [16, 2, 128, 128], P('space', 'grp'), may hold values from -0.4 to 0.4
- x_coupling: float32 [16, 2, 128, 128], P('space', 'grp'), may hold values from -0.35 to 0.35
- y_coupling: float32 [16, 2, 128, 128], P('space', 'grp'), may hold values from -0.35 to 0.35
- levels: float32 [16, 2, 128], P('space', 'grp'), may hold values from -2 to 2
- listed: int32 [16, 2, 2], P('space', 'grp'), may hold values 0 or 1
Outputs:
- density_diag: float32 [16, 2, 128, 128], P('space', 'grp')
- density_x: float32 [16, 2, 128, 128], P('space', 'grp')
- density_y: float32 [16, 2, 128, 128], P('space', 'grp')
The draws below stay inside these ranges and needn't reach their ends.
Inputs may be any that keep to these rules, and one draw needn't show every extreme that they name: listed[i,j,0] keeps the coupling of block (i,j) with (i+1,j), listed[i,j,1] that with (i,j+1).
All inputs are finite; a program needn't handle non-finite values.
Results may differ from the reference program's by a relative error of at most 0.0037.
Values sent between devices are 32-bit elements; how exact they have to be, the bound alone decides.
A program may use at most 64 MiB of HBM per device.

```python
import jax
import jax.numpy as jnp
from jax import lax

BLK = 128
NX = 16
NY = 2


def set_ends(entries, stream_key, low, largest):
    dims = entries.shape
    place = [jax.random.randint(jax.random.fold_in(stream_key, axis), (), 0, dims[axis]) for axis in range(len(dims))]
    entries = entries.at[tuple(place)].set(low)
    longest = dims.index(max(dims))
    place[longest] = (place[longest] + 1) % dims[longest]
    return entries.at[tuple(place)].set(largest)


def steps_of(stream_key, shape, shards, low, top_value):
    factor_of, own = 1.0, jax.random.fold_in(stream_key, 6)
    for position, shards_of in shards:
        draws = jnp.exp(jax.random.uniform(jax.random.fold_in(own, position), (shards_of,), jnp.float32, low / len(shards), top_value / len(shards)))
        factor_of = factor_of * jnp.repeat(draws, shape[position] // shards_of).reshape([-1 if axis == position else 1 for axis in range(len(shape))])
    return factor_of


def normal_values(own_key, dims, deviation, limit, shards=(), kind=jnp.bfloat16):
    loudness = steps_of(own_key, dims, shards, -0.22, 0.18) if shards else 1.0
    values = jax.random.normal(own_key, dims, jnp.float32) * deviation * loudness
    return jnp.minimum(jnp.maximum(values, -limit), limit).astype(kind)


def setup_inputs(seed: int = 0) -> dict:
    seeds = jax.random.split(jax.random.key(seed), 6)
    diag_blocks = normal_values(seeds[0], (NX, NY, BLK, BLK), 0.06, 0.4, ((0, 16), (1, 2)), jnp.float32)
    x_coupling = normal_values(seeds[1], (NX, NY, BLK, BLK), 0.05, 0.35, ((0, 16), (1, 2)), jnp.float32)
    y_coupling = normal_values(seeds[2], (NX, NY, BLK, BLK), 0.05, 0.35, ((0, 16), (1, 2)), jnp.float32)
    levels = jnp.clip(jax.random.uniform(seeds[3], (NX, NY, BLK), jnp.float32, -2.0, 2.0) * steps_of(seeds[3], (NX, NY, BLK), ((0, 16), (1, 2)), -0.4, 0.0), -2.0, 2.0)
    listed = set_ends((jax.random.randint(seeds[4], (NX, NY, 2), 0, 4) < 3).astype(jnp.int32), jax.random.fold_in(seeds[4], 1), 0, 1)
    return {"diag_blocks": diag_blocks, "x_coupling": x_coupling, "y_coupling": y_coupling, "levels": levels, "listed": listed}


hubbard = 1.0

def symmetric(matrix):
    return 0.5 * (matrix + matrix.T)

def assemble(center, nbr_diag, nbr_coup):
    block_width = center.shape[0]
    zero_block = jnp.zeros((block_width, block_width), center.dtype)
    top_row = jnp.concatenate([center] + [nbr_coup[member].T for member in range(4)], axis=1)
    row_list = [top_row]
    for member in range(4):
        pieces = [nbr_coup[member]] + [nbr_diag[member] if column_slot == member else zero_block for column_slot in range(4)]
        row_list.append(jnp.concatenate(pieces, axis=1))
    return jnp.concatenate(row_list, axis=0)

def density_column(matrix):
    order_size = matrix.shape[0]
    block_width = order_size // 5
    matrix_half = matrix.astype(jnp.bfloat16)
    square = jnp.dot(matrix_half, matrix_half, preferred_element_type=jnp.float32)
    square_half = square.astype(jnp.bfloat16)
    fourth = jnp.dot(square_half, square_half, preferred_element_type=jnp.float32)
    scale_four = jnp.sqrt(jnp.sum(fourth * fourth) + 1e-06)
    scale_two = jnp.sqrt(scale_four)
    scale_one = jnp.sqrt(scale_two)
    identity = jnp.eye(order_size, dtype=jnp.float32)
    initial = (matrix / scale_one).astype(jnp.bfloat16)
    factor = (3.0 * identity - square / scale_two).astype(jnp.bfloat16)
    iterate = (0.5 * jnp.dot(initial, factor, preferred_element_type=jnp.float32)).astype(jnp.bfloat16)
    column = iterate[:, :block_width]
    applied_once = jnp.dot(iterate, column, preferred_element_type=jnp.float32).astype(jnp.bfloat16)
    applied_twice = jnp.dot(iterate, applied_once, preferred_element_type=jnp.float32)
    sign_part = 0.5 * (3.0 * column.astype(jnp.float32) - applied_twice)
    density = 0.5 * (identity[:, :block_width] - sign_part)
    return density.reshape(5, block_width, block_width)

def sweep(diag_all, x_all, y_all):
    size_x = diag_all.shape[0]
    size_y = diag_all.shape[1]
    block_width = diag_all.shape[2]
    widths = ((1, 1), (1, 1), (0, 0), (0, 0))
    pad_diag = jnp.pad(diag_all, widths)
    pad_x = jnp.pad(x_all, widths)
    pad_y = jnp.pad(y_all, widths)
    zero_index = jnp.int32(0)

    def one_site(flat):
        row_index = flat // size_y
        col_index = flat % size_y

        def pick(array, shift_x, shift_y):
            start_x = (row_index + (1 + shift_x)).astype(jnp.int32)
            start_y = (col_index + (1 + shift_y)).astype(jnp.int32)
            return lax.dynamic_slice(array, (start_x, start_y, zero_index, zero_index), (1, 1, block_width, block_width))[0, 0]
        center = pick(pad_diag, 0, 0)
        nbr_diag = jnp.stack([pick(pad_diag, -1, 0), pick(pad_diag, 1, 0), pick(pad_diag, 0, -1), pick(pad_diag, 0, 1)])
        nbr_coup = jnp.stack([pick(pad_x, -1, 0), pick(pad_x, 0, 0).T, pick(pad_y, 0, -1), pick(pad_y, 0, 0).T])
        return density_column(assemble(center, nbr_diag, nbr_coup))
    columns = lax.map(one_site, jnp.arange(size_x * size_y, dtype=jnp.int32))
    columns = columns.reshape(size_x, size_y, 5, block_width, block_width)
    diag_density = 0.5 * (columns[:, :, 0] + jnp.swapaxes(columns[:, :, 0], -1, -2))
    from_x = jnp.concatenate([columns[1:, :, 1], jnp.zeros_like(columns[:1, :, 1])], axis=0)
    x_density = 0.5 * (jnp.swapaxes(columns[:, :, 2], -1, -2) + from_x)
    from_y = jnp.concatenate([columns[:, 1:, 3], jnp.zeros_like(columns[:, :1, 3])], axis=1)
    y_density = 0.5 * (jnp.swapaxes(columns[:, :, 4], -1, -2) + from_y)
    return (diag_density, x_density, y_density)

def reference(diag_blocks, x_coupling, y_coupling, levels, listed):
    identity = jnp.eye(BLK, dtype=jnp.float32)
    pos_x = jnp.arange(NX, dtype=jnp.int32)[:, None]
    pos_y = jnp.arange(NY, dtype=jnp.int32)[None, :]
    flag_x = listed[:, :, 0].astype(jnp.float32) * (pos_x < NX - 1).astype(jnp.float32)
    flag_y = listed[:, :, 1].astype(jnp.float32) * (pos_y < NY - 1).astype(jnp.float32)
    onsite = 0.5 * (diag_blocks + jnp.swapaxes(diag_blocks, -1, -2)) + levels[..., None] * identity
    coup_x = x_coupling * flag_x[:, :, None, None]
    coup_y = y_coupling * flag_y[:, :, None, None]
    diag_one, x_one, y_one = sweep(onsite, coup_x, coup_y)
    onsite_two = onsite + hubbard * (diag_one - 0.5 * identity)
    coup_x_two = coup_x + hubbard * x_one
    coup_y_two = coup_y + hubbard * y_one
    diag_two, x_two, y_two = sweep(onsite_two, coup_x_two, coup_y_two)
    return (diag_two, x_two, y_two)
```

```python
import functools

import jax
import jax.numpy as jnp
from jax import lax
from jax.experimental import pallas as pl
from jax.experimental.pallas import tpu as pltpu
from jax.sharding import PartitionSpec as P

hubbard = 1.0
MESH = pl.DeviceIdType.MESH
F32 = jnp.float32
BF16 = jnp.bfloat16


def mm(a, b):
    return jnp.dot(a, b, preferred_element_type=F32)


def eye(w):
    return lax.broadcasted_iota(jnp.int32, (w, w), 0) == lax.broadcasted_iota(jnp.int32, (w, w), 1)


def density_columns(w, row0, v1, dk, sx, fb, w13, v3, v5, v7, v5b, v1f, cols):
    n = 5 * w

    def bl(i):
        return slice(i * w, (i + 1) * w)

    d0 = row0[:, bl(0)]
    sx[:, n:] = v1[...]
    w13[:, :w] = v1[...]
    sx[bl(0), bl(0)] = mm(row0[...], v1[...]).astype(BF16)
    for half in range(2):
        t = mm(v1[w:, :], row0[:, w * (1 + 2 * half) : w * (3 + 2 * half)])
        for l in (0, 1):
            k = 2 * half + l
            for r in range(4):
                piece = t[bl(r), bl(l)]
                if r == k:
                    piece = piece + mm(dk[k], dk[k])
                sx[bl(1 + r), bl(1 + k)] = piece.astype(BF16)
    for k in range(4):
        bk, btk = v1[bl(1 + k), :], row0[:, bl(1 + k)]
        sx[bl(1 + k), bl(0)] = (mm(bk, d0) + mm(dk[k], bk)).astype(BF16)
        sx[bl(0), bl(1 + k)] = (mm(d0, btk) + mm(btk, dk[k])).astype(BF16)
    total = jnp.zeros((1, 2 * w), F32)
    for c in range(3):
        f = mm(sx[:, :n], sx[:, 2 * w * c : 2 * w * (c + 1)])
        if c == 2:
            v3[...] = f[:, w:]
            w13[:, w:] = f[:, w:].astype(BF16)
            f = f[:, :w]
            fb[:, 4 * w :] = f.astype(BF16)
            last = jnp.sum(f * f, axis=0, keepdims=True)
        else:
            fb[:, 2 * w * c : 2 * w * (c + 1)] = f.astype(BF16)
            total = total + jnp.sum(f * f, axis=0, keepdims=True)
    g = mm(fb[...], w13[...])
    v5[...] = g[:, :w]
    v5b[...] = g[:, :w].astype(BF16)
    v7[...] = g[:, w:]
    v9 = mm(fb[...], v5b[...])
    squares = jnp.sum(total, axis=1, keepdims=True) + jnp.sum(last, axis=1, keepdims=True)
    scale_two = jnp.sqrt(jnp.sqrt(squares + 1e-06))
    scale_one = jnp.sqrt(scale_two)
    al = 1.5 / scale_one
    be = 0.5 / (scale_one * scale_two)
    c1 = -0.75 * al
    c3 = 0.75 * be + 0.25 * al * al * al
    c5 = -0.75 * al * al * be
    c7 = 0.75 * al * be * be
    c9 = -0.25 * be * be * be
    res = c1 * v1f[...] + c3 * v3[...] + c5 * v5[...] + c7 * v7[...] + c9 * v9
    cols[...] = res
    cols[bl(0), :] = res[bl(0), :] + jnp.where(eye(w), 0.5, 0.0)


def kernel(
    sizes, diag_hbm, x_hbm, y_hbm, lev_hbm, list_hbm, od_ref, ox_ref, oy_ref,
    din, xin, yin, lin, fin, in_sems,
    send1, rd1, rb1, send2, rd2, rc2, rf3,
    row0, v1, dk, sx, fb, w13, v3, v5, v7, v5b, v1f, cols,
    send_sems, recv_sems,
):
    nx, ny = sizes
    w = din.shape[0]
    ix = lax.axis_index("space")
    iy = lax.axis_index("grp")
    has = [ix > 0, ix < nx - 1, iy > 0, iy < ny - 1]
    dev = [
        (jnp.maximum(ix - 1, 0), iy),
        (jnp.minimum(ix + 1, nx - 1), iy),
        (ix, jnp.maximum(iy - 1, 0)),
        (ix, jnp.minimum(iy + 1, ny - 1)),
    ]

    def bl(i):
        return slice(i * w, (i + 1) * w)

    barrier = pltpu.get_barrier_semaphore()
    for k in range(4):
        @pl.when(has[k])
        def _():
            pl.semaphore_signal(barrier, inc=1, device_id=dev[k], device_id_type=MESH)

    loads = [
        pltpu.make_async_copy(diag_hbm.at[0, 0], din, in_sems.at[0]),
        pltpu.make_async_copy(x_hbm.at[0, 0], xin, in_sems.at[1]),
        pltpu.make_async_copy(y_hbm.at[0, 0], yin, in_sems.at[2]),
        pltpu.make_async_copy(lev_hbm.at[0], lin, in_sems.at[3]),
        pltpu.make_async_copy(list_hbm.at[0], fin, in_sems.at[4]),
    ]
    for load in loads:
        load.start()
    for k in range(4):
        @pl.when(jnp.logical_not(has[k]))
        def _():
            zero = jnp.zeros((w, w), F32)
            rd1[k] = zero
            rd2[k] = zero
            rc2[k] = zero
            if k % 2 == 0:
                rb1[k // 2] = zero
            else:
                rf3[k // 2] = zero
    for load in loads:
        load.wait()
    one_eye = eye(w)
    flag_x = fin[0, 0].astype(F32) * (ix < nx - 1).astype(F32)
    flag_y = fin[0, 1].astype(F32) * (iy < ny - 1).astype(F32)
    raw = din[...]
    onsite = 0.5 * (raw + raw.T) + jnp.where(one_eye, jnp.broadcast_to(lin[...], (w, w)), 0.0)
    send1[0] = onsite
    send1[1] = xin[...] * flag_x
    send1[2] = yin[...] * flag_y

    count = sum(h.astype(jnp.int32) for h in has)
    pl.semaphore_wait(barrier, count)

    def transfer(src, dst, index_send, index_recv, k):
        return pltpu.make_async_remote_copy(
            src_ref=src, dst_ref=dst, send_sem=send_sems.at[index_send],
            recv_sem=recv_sems.at[index_recv], device_id=dev[k], device_id_type=MESH,
        )

    def diag1(k):
        return transfer(send1.at[0], rd1.at[k ^ 1], k, k ^ 1, k)

    def coup1(k):
        return transfer(send1.at[1 + k // 2], rb1.at[k // 2], 4 + k // 2, 4 + k // 2, k)

    def diag2(k):
        return transfer(send2, rd2.at[k ^ 1], 6 + k, 6 + (k ^ 1), k)

    def coup2(k):
        return transfer(cols1.at[bl(1 + k), :], rc2.at[k ^ 1], 10 + k, 10 + (k ^ 1), k)

    def coup3(k):
        return transfer(cols2.at[bl(1 + k), :], rf3.at[k // 2], 14 + k // 2, 14 + k // 2, k)

    cols1, cols2 = cols.at[0], cols.at[1]

    order = (3, 2, 1, 0)
    for k in order:
        @pl.when(has[k])
        def _():
            if k % 2:
                coup1(k).start()
            diag1(k).start()

    row0[:, bl(0)] = onsite.astype(BF16)
    v1[bl(0), :] = onsite.astype(BF16)
    v1f[bl(0), :] = onsite
    for axis in range(2):
        coup = send1[1 + axis]
        coup_t = coup.T
        row0[:, bl(2 + 2 * axis)] = coup.astype(BF16)
        v1[bl(2 + 2 * axis), :] = coup_t.astype(BF16)
        v1f[bl(2 + 2 * axis), :] = coup_t
    for k in (0, 1, 2, 3):
        @pl.when(has[k])
        def _():
            if k % 2 == 0:
                coup1(k ^ 1).wait_recv()
            diag1(k ^ 1).wait_recv()
    for k in range(4):
        dk[k] = rd1[k].astype(BF16)
    for axis in range(2):
        coup = rb1[axis]
        row0[:, bl(1 + 2 * axis)] = coup.T.astype(BF16)
        v1[bl(1 + 2 * axis), :] = coup.astype(BF16)
        v1f[bl(1 + 2 * axis), :] = coup

    density_columns(w, row0, v1, dk, sx, fb, w13, v3, v5, v7, v5b, v1f, cols1)

    for k in order:
        @pl.when(has[k])
        def _():
            coup2(k).start()
    c0 = cols1[bl(0), :]
    onsite_two = v1f[bl(0), :] + hubbard * (0.5 * (c0 + c0.T) - jnp.where(one_eye, 0.5, 0.0))
    send2[...] = onsite_two
    for k in order:
        @pl.when(has[k])
        def _():
            diag2(k).start()
    row0[:, bl(0)] = onsite_two.astype(BF16)
    v1[bl(0), :] = onsite_two.astype(BF16)
    v1f[bl(0), :] = onsite_two
    for k in range(4):
        v1f[bl(1 + k), :] = v1f[bl(1 + k), :] + 0.5 * hubbard * cols1[bl(1 + k), :]
    for k in (0, 1, 2, 3):
        @pl.when(has[k])
        def _():
            coup2(k ^ 1).wait_recv()
            diag2(k ^ 1).wait_recv()
    for k in range(4):
        dk[k] = rd2[k].astype(BF16)
        bk = v1f[bl(1 + k), :] + 0.5 * hubbard * rc2[k].T
        v1f[bl(1 + k), :] = bk
        v1[bl(1 + k), :] = bk.astype(BF16)
        row0[:, bl(1 + k)] = bk.T.astype(BF16)

    density_columns(w, row0, v1, dk, sx, fb, w13, v3, v5, v7, v5b, v1f, cols2)

    for k in (2, 0):
        @pl.when(has[k])
        def _():
            coup3(k).start()
    c0 = cols2[bl(0), :]
    od_ref[0, 0] = 0.5 * (c0 + c0.T)
    ox_ref[0, 0] = 0.5 * cols2[bl(2), :].T
    oy_ref[0, 0] = 0.5 * cols2[bl(4), :].T
    for k in (1, 3):
        @pl.when(has[k])
        def _():
            coup3(k ^ 1).wait_recv()
    ox_ref[0, 0] = ox_ref[0, 0] + 0.5 * rf3[0]
    oy_ref[0, 0] = oy_ref[0, 0] + 0.5 * rf3[1]
    for k in range(4):
        @pl.when(has[k])
        def _():
            if k % 2:
                coup1(k).wait_send()
            else:
                coup3(k).wait_send()
            diag1(k).wait_send()
            coup2(k).wait_send()
            diag2(k).wait_send()


def per_device(diag_blocks, x_coupling, y_coupling, levels, listed):
    w = diag_blocks.shape[-1]
    n = 5 * w
    sizes = (lax.axis_size("space"), lax.axis_size("grp"))
    block = jax.ShapeDtypeStruct((1, 1, w, w), F32)
    any_spec = pl.BlockSpec(memory_space=pl.ANY)
    vmem_spec = pl.BlockSpec(memory_space=pltpu.VMEM)
    return pl.pallas_call(
        functools.partial(kernel, sizes),
        out_shape=(block, block, block),
        in_specs=[any_spec] * 5,
        out_specs=(vmem_spec,) * 3,
        scratch_shapes=[
            pltpu.VMEM((w, w), F32),
            pltpu.VMEM((w, w), F32),
            pltpu.VMEM((w, w), F32),
            pltpu.VMEM((1, w), F32),
            pltpu.SMEM((1, 2), jnp.int32),
            pltpu.SemaphoreType.DMA((5,)),
            pltpu.VMEM((3, w, w), F32),
            pltpu.VMEM((4, w, w), F32),
            pltpu.VMEM((2, w, w), F32),
            pltpu.VMEM((w, w), F32),
            pltpu.VMEM((4, w, w), F32),
            pltpu.VMEM((4, w, w), F32),
            pltpu.VMEM((2, w, w), F32),
            pltpu.VMEM((w, n), BF16),
            pltpu.VMEM((n, w), BF16),
            pltpu.VMEM((4, w, w), BF16),
            pltpu.VMEM((n, n + w), BF16),
            pltpu.VMEM((n, n), BF16),
            pltpu.VMEM((n, 2 * w), BF16),
            pltpu.VMEM((n, w), F32),
            pltpu.VMEM((n, w), F32),
            pltpu.VMEM((n, w), F32),
            pltpu.VMEM((n, w), BF16),
            pltpu.VMEM((n, w), F32),
            pltpu.VMEM((2, n, w), F32),
            pltpu.SemaphoreType.DMA((16,)),
            pltpu.SemaphoreType.DMA((16,)),
        ],
        compiler_params=pltpu.CompilerParams(collective_id=0, has_side_effects=True),
    )(diag_blocks, x_coupling, y_coupling, levels, listed)


def solution(mesh):
    blocks = P("space", "grp", None, None)
    rows = P("space", "grp", None)
    return jax.shard_map(
        per_device,
        mesh=mesh,
        in_specs=(blocks, blocks, blocks, rows, rows),
        out_specs=(blocks, blocks, blocks),
        check_vma=False,
    )
```

```python
import functools

import jax
import jax.numpy as jnp
from jax import lax
from jax.experimental import pallas as pl
from jax.experimental.pallas import tpu as pltpu
from jax.sharding import PartitionSpec as P

hubbard = 1.0
MESH = pl.DeviceIdType.MESH
F32 = jnp.float32
BF16 = jnp.bfloat16


def mm(a, b):
    return jnp.dot(a, b, preferred_element_type=F32)


def eye(w):
    return lax.broadcasted_iota(jnp.int32, (w, w), 0) == lax.broadcasted_iota(jnp.int32, (w, w), 1)


def density_columns(w, row0, v1, dk, sx, fb, v3, u, v1f, cols, after_x, arrived):
    n = 5 * w

    def bl(i):
        return slice(i * w, (i + 1) * w)

    d0 = row0[:, bl(0)]
    for k in arrived(range(4)):
        top = jnp.concatenate([d0, row0[:, bl(1 + k)]], axis=1)
        low = jnp.concatenate([v1[bl(1 + k), :], dk[k]], axis=1)
        pair = jnp.concatenate([top, low], axis=0)
        part = mm(pair, pair).astype(BF16)
        sx[bl(0), bl(1 + k)] = part[:w, w:]
        sx[bl(1 + k), bl(0)] = part[w:, :w]
        sx[bl(1 + k), bl(1 + k)] = part[w:, w:]
    sx[bl(0), bl(0)] = mm(row0[...], v1[...]).astype(BF16)
    for half in range(2):
        t = mm(v1[w:, :], row0[:, w * (1 + 2 * half) : w * (3 + 2 * half)])
        for l in (0, 1):
            k = 2 * half + l
            for r in range(4):
                if r != k:
                    sx[bl(1 + r), bl(1 + k)] = t[bl(r), bl(l)].astype(BF16)
    first = mm(row0[...], sx[:, bl(0)])
    v3[bl(0), :] = first
    sx[bl(0), n:] = first.astype(BF16)
    for k in range(4):
        low = jnp.concatenate([v1[bl(1 + k), :], dk[k]], axis=1)
        vec = jnp.concatenate([sx[bl(0), bl(0)], sx[bl(1 + k), bl(0)]], axis=0)
        first = mm(low, vec)
        v3[bl(1 + k), :] = first
        sx[bl(1 + k), n:] = first.astype(BF16)
    total = jnp.zeros((1, 2 * w), F32)
    for c in range(2):
        f = mm(sx[:, :n], sx[:, 2 * w * c : 2 * w * (c + 1)])
        fb[:, 2 * w * c : 2 * w * (c + 1)] = f.astype(BF16)
        total = total + jnp.sum(f * f, axis=0, keepdims=True)
    f = mm(sx[:, :n], sx[:, 4 * w :])
    v5 = f[:, w:]
    f = f[:, :w]
    fb[:, 4 * w :] = f.astype(BF16)
    total = total[:, :w] + total[:, w:] + jnp.sum(f * f, axis=0, keepdims=True)
    squares = jnp.sum(total, axis=1, keepdims=True)
    scale_two = jnp.sqrt(jnp.sqrt(squares + 1e-06))
    scale_one = jnp.sqrt(scale_two)
    al = 1.5 / scale_one
    be = 0.5 / (scale_one * scale_two)
    c1 = -0.75 * al
    c3 = 0.75 * be + 0.25 * al * al * al
    c5 = -0.75 * al * al * be
    c7 = 0.75 * al * be * be
    c9 = -0.25 * be * be * be
    u[...] = (c5 * v1f[...] + c7 * v3[...] + c9 * v5).astype(BF16)
    top = slice(0, 3 * w)
    cols[top, :] = mm(fb[top, :], u[...]) + (c1 * v1f[top, :] + c3 * v3[top, :])
    cols[bl(0), :] = cols[bl(0), :] + jnp.where(eye(w), 0.5, 0.0)
    after_x()
    top = slice(3 * w, n)
    cols[top, :] = mm(fb[top, :], u[...]) + (c1 * v1f[top, :] + c3 * v3[top, :])


def kernel(
    sizes, diag_hbm, x_hbm, y_hbm, lev_hbm, list_hbm, out_ref,
    din, xin, yin, lin, fin, in_sems,
    send1, rd1, rb1, send2, rd2, rc2, rf3,
    row0, v1, dk, sx, fb, v3, u, v1f, cols,
    send_sems, recv_sems,
):
    nx, ny = sizes
    w = din.shape[0]
    ix = lax.axis_index("space")
    iy = lax.axis_index("grp")
    has = [ix > 0, ix < nx - 1, iy > 0, iy < ny - 1]
    dev = [
        (jnp.maximum(ix - 1, 0), iy),
        (jnp.minimum(ix + 1, nx - 1), iy),
        (ix, jnp.maximum(iy - 1, 0)),
        (ix, jnp.minimum(iy + 1, ny - 1)),
    ]

    def bl(i):
        return slice(i * w, (i + 1) * w)

    barrier = pltpu.get_barrier_semaphore()
    for k in range(4):
        @pl.when(has[k])
        def _():
            pl.semaphore_signal(barrier, inc=1, device_id=dev[k], device_id_type=MESH)

    loads = [
        pltpu.make_async_copy(diag_hbm.at[0, 0], din, in_sems.at[0]),
        pltpu.make_async_copy(x_hbm.at[0, 0], xin, in_sems.at[1]),
        pltpu.make_async_copy(y_hbm.at[0, 0], yin, in_sems.at[2]),
        pltpu.make_async_copy(lev_hbm.at[0], lin, in_sems.at[3]),
        pltpu.make_async_copy(list_hbm.at[0], fin, in_sems.at[4]),
    ]
    for load in loads:
        load.start()
    for k in range(4):
        @pl.when(jnp.logical_not(has[k]))
        def _():
            zero = jnp.zeros((w, w), F32)
            rd1[k] = zero
            rd2[k] = zero
            rc2[k] = zero
            if k % 2 == 0:
                rb1[k // 2] = zero
            else:
                rf3[k // 2] = zero
    for load in loads:
        load.wait()
    one_eye = eye(w)
    flag_x = fin[0, 0].astype(F32) * (ix < nx - 1).astype(F32)
    flag_y = fin[0, 1].astype(F32) * (iy < ny - 1).astype(F32)
    raw = din[...]
    onsite = 0.5 * (raw + raw.T) + jnp.where(one_eye, jnp.broadcast_to(lin[...], (w, w)), 0.0)
    send1[0] = onsite
    send1[1] = xin[...] * flag_x
    send1[2] = yin[...] * flag_y

    count = sum(h.astype(jnp.int32) for h in has)
    pl.semaphore_wait(barrier, count)

    def transfer(src, dst, index_send, index_recv, k):
        return pltpu.make_async_remote_copy(
            src_ref=src, dst_ref=dst, send_sem=send_sems.at[index_send],
            recv_sem=recv_sems.at[index_recv], device_id=dev[k], device_id_type=MESH,
        )

    def diag1(k):
        return transfer(send1.at[0], rd1.at[k ^ 1], k, k ^ 1, k)

    def coup1(k):
        return transfer(send1.at[1 + k // 2], rb1.at[k // 2], 4 + k // 2, 4 + k // 2, k)

    def diag2(k):
        return transfer(send2, rd2.at[k ^ 1], 6 + k, 6 + (k ^ 1), k)

    def coup2(k):
        return transfer(cols1.at[bl(1 + k), :], rc2.at[k ^ 1], 10 + k, 10 + (k ^ 1), k)

    def coup3(k):
        return transfer(cols2.at[bl(1 + k), :], rf3.at[k // 2], 14 + k // 2, 14 + k // 2, k)

    cols1, cols2 = cols.at[0], cols.at[1]

    order = (1, 0, 3, 2)
    for k in order:
        @pl.when(has[k])
        def _():
            if k % 2:
                coup1(k).start()
            diag1(k).start()

    row0[:, bl(0)] = onsite.astype(BF16)
    v1[bl(0), :] = onsite.astype(BF16)
    v1f[bl(0), :] = onsite
    for axis in range(2):
        coup = send1[1 + axis]
        coup_t = coup.T
        row0[:, bl(2 + 2 * axis)] = coup.astype(BF16)
        v1[bl(2 + 2 * axis), :] = coup_t.astype(BF16)
        v1f[bl(2 + 2 * axis), :] = coup_t
    def arrived1(slots):
        for k in (2, 3, 1, 0):
            @pl.when(has[k])
            def _():
                if k % 2 == 0:
                    coup1(k ^ 1).wait_recv()
                diag1(k ^ 1).wait_recv()
            dk[k] = rd1[k].astype(BF16)
            if k % 2 == 0:
                coup = rb1[k // 2]
                row0[:, bl(1 + k)] = coup.T.astype(BF16)
                v1[bl(1 + k), :] = coup.astype(BF16)
                v1f[bl(1 + k), :] = coup
            yield k

    onsite_two = []

    def send_x2():
        for k in (1, 0):
            @pl.when(has[k])
            def _():
                coup2(k).start()
        c0 = cols1[bl(0), :]
        two = v1f[bl(0), :] + hubbard * (0.5 * (c0 + c0.T) - jnp.where(one_eye, 0.5, 0.0))
        send2[...] = two
        onsite_two.append(two)
        for k in order:
            @pl.when(has[k])
            def _():
                diag2(k).start()

    density_columns(w, row0, v1, dk, sx, fb, v3, u, v1f, cols1, send_x2, arrived1)

    for k in (3, 2):
        @pl.when(has[k])
        def _():
            coup2(k).start()
    two = onsite_two[0]
    row0[:, bl(0)] = two.astype(BF16)
    v1[bl(0), :] = two.astype(BF16)
    v1f[bl(0), :] = two
    for k in range(4):
        v1f[bl(1 + k), :] = v1f[bl(1 + k), :] + 0.5 * hubbard * cols1[bl(1 + k), :]

    def arrived2(slots):
        for k in (2, 3, 1, 0):
            @pl.when(has[k])
            def _():
                coup2(k ^ 1).wait_recv()
                diag2(k ^ 1).wait_recv()
            dk[k] = rd2[k].astype(BF16)
            bk = v1f[bl(1 + k), :] + 0.5 * hubbard * rc2[k].T
            v1f[bl(1 + k), :] = bk
            v1[bl(1 + k), :] = bk.astype(BF16)
            row0[:, bl(1 + k)] = bk.T.astype(BF16)
            yield k

    def send_x3():
        @pl.when(has[0])
        def _():
            coup3(0).start()

    density_columns(w, row0, v1, dk, sx, fb, v3, u, v1f, cols2, send_x3, arrived2)

    @pl.when(has[2])
    def _():
        coup3(2).start()
    c0 = cols2[bl(0), :]
    out_ref[0] = 0.5 * (c0 + c0.T)
    half_x = 0.5 * cols2[bl(2), :].T
    half_y = 0.5 * cols2[bl(4), :].T
    for k in (3, 1):
        @pl.when(has[k])
        def _():
            coup3(k ^ 1).wait_recv()
    out_ref[1] = half_x + 0.5 * rf3[0]
    out_ref[2] = half_y + 0.5 * rf3[1]
    for k in range(4):
        @pl.when(has[k])
        def _():
            if k % 2:
                coup1(k).wait_send()
            else:
                coup3(k).wait_send()
            diag1(k).wait_send()
            coup2(k).wait_send()
            diag2(k).wait_send()


def write_out(in_ref, od_ref, ox_ref, oy_ref, sems):
    copies = [
        pltpu.make_async_copy(in_ref.at[i], ref.at[0, 0], sems.at[i])
        for i, ref in enumerate((od_ref, ox_ref, oy_ref))
    ]
    for copy in copies:
        copy.start()
    for copy in copies:
        copy.wait()


def per_device(diag_blocks, x_coupling, y_coupling, levels, listed):
    w = diag_blocks.shape[-1]
    n = 5 * w
    sizes = (lax.axis_size("space"), lax.axis_size("grp"))
    block = jax.ShapeDtypeStruct((1, 1, w, w), F32)
    any_spec = pl.BlockSpec(memory_space=pl.ANY)
    vmem_spec = pl.BlockSpec(memory_space=pltpu.VMEM)
    results = pl.pallas_call(
        functools.partial(kernel, sizes),
        out_shape=pltpu.VMEM((3, w, w), F32),
        in_specs=[any_spec] * 5,
        out_specs=vmem_spec,
        scratch_shapes=[
            pltpu.VMEM((w, w), F32),
            pltpu.VMEM((w, w), F32),
            pltpu.VMEM((w, w), F32),
            pltpu.VMEM((1, w), F32),
            pltpu.SMEM((1, 2), jnp.int32),
            pltpu.SemaphoreType.DMA((5,)),
            pltpu.VMEM((3, w, w), F32),
            pltpu.VMEM((4, w, w), F32),
            pltpu.VMEM((2, w, w), F32),
            pltpu.VMEM((w, w), F32),
            pltpu.VMEM((4, w, w), F32),
            pltpu.VMEM((4, w, w), F32),
            pltpu.VMEM((2, w, w), F32),
            pltpu.VMEM((w, n), BF16),
            pltpu.VMEM((n, w), BF16),
            pltpu.VMEM((4, w, w), BF16),
            pltpu.VMEM((n, n + w), BF16),
            pltpu.VMEM((n, n), BF16),
            pltpu.VMEM((n, w), F32),
            pltpu.VMEM((n, w), BF16),
            pltpu.VMEM((n, w), F32),
            pltpu.VMEM((2, n, w), F32),
            pltpu.SemaphoreType.DMA((16,)),
            pltpu.SemaphoreType.DMA((16,)),
        ],
        compiler_params=pltpu.CompilerParams(collective_id=0, has_side_effects=True),
    )(diag_blocks, x_coupling, y_coupling, levels, listed)
    return pl.pallas_call(
        write_out,
        out_shape=(block, block, block),
        in_specs=[vmem_spec],
        out_specs=(any_spec,) * 3,
        scratch_shapes=[pltpu.SemaphoreType.DMA((3,))],
    )(results)


def solution(mesh):
    blocks = P("space", "grp", None, None)
    rows = P("space", "grp", None)
    return jax.shard_map(
        per_device,
        mesh=mesh,
        in_specs=(blocks, blocks, blocks, rows, rows),
        out_specs=(blocks, blocks, blocks),
        check_vma=False,
    )
```

```python
import functools

import jax
import jax.numpy as jnp
from jax import lax
from jax.experimental import pallas as pl
from jax.experimental.pallas import tpu as pltpu
from jax.sharding import PartitionSpec as P

hubbard = 1.0
MESH = pl.DeviceIdType.MESH
F32 = jnp.float32
BF16 = jnp.bfloat16


def mm(a, b):
    return jnp.dot(a, b, preferred_element_type=F32)


def eye(w):
    return lax.broadcasted_iota(jnp.int32, (w, w), 0) == lax.broadcasted_iota(jnp.int32, (w, w), 1)


def density_columns(w, row0, v1, dk, sx, fb, v3, u, v1f, cols, after_x, arrived):
    n = 5 * w

    def bl(i):
        return slice(i * w, (i + 1) * w)

    d0 = row0[:, bl(0)]
    for k in arrived(range(4)):
        top = jnp.concatenate([d0, row0[:, bl(1 + k)]], axis=1)
        low = jnp.concatenate([v1[bl(1 + k), :], dk[k]], axis=1)
        pair = jnp.concatenate([top, low], axis=0)
        part = mm(pair, pair).astype(BF16)
        sx[bl(0), bl(1 + k)] = part[:w, w:]
        sx[bl(1 + k), bl(0)] = part[w:, :w]
        sx[bl(1 + k), bl(1 + k)] = part[w:, w:]
    sx[bl(0), bl(0)] = mm(row0[...], v1[...]).astype(BF16)
    for half in range(2):
        t = mm(v1[w:, :], row0[:, w * (1 + 2 * half) : w * (3 + 2 * half)])
        for l in (0, 1):
            k = 2 * half + l
            for r in range(4):
                if r != k:
                    sx[bl(1 + r), bl(1 + k)] = t[bl(r), bl(l)].astype(BF16)
    first = mm(row0[...], sx[:, bl(0)])
    v3[bl(0), :] = first
    sx[bl(0), n:] = first.astype(BF16)
    for k in range(4):
        low = jnp.concatenate([v1[bl(1 + k), :], dk[k]], axis=1)
        vec = jnp.concatenate([sx[bl(0), bl(0)], sx[bl(1 + k), bl(0)]], axis=0)
        first = mm(low, vec)
        v3[bl(1 + k), :] = first
        sx[bl(1 + k), n:] = first.astype(BF16)
    total = jnp.zeros((1, 2 * w), F32)
    for c in range(2):
        f = mm(sx[:, :n], sx[:, 2 * w * c : 2 * w * (c + 1)])
        fb[:, 2 * w * c : 2 * w * (c + 1)] = f.astype(BF16)
        total = total + jnp.sum(f * f, axis=0, keepdims=True)
    f = mm(sx[:, :n], sx[:, 4 * w :])
    v5 = f[:, w:]
    f = f[:, :w]
    fb[:, 4 * w :] = f.astype(BF16)
    total = total[:, :w] + total[:, w:] + jnp.sum(f * f, axis=0, keepdims=True)
    squares = jnp.sum(total, axis=1, keepdims=True)
    scale_two = jnp.sqrt(jnp.sqrt(squares + 1e-06))
    scale_one = jnp.sqrt(scale_two)
    al = 1.5 / scale_one
    be = 0.5 / (scale_one * scale_two)
    c1 = -0.75 * al
    c3 = 0.75 * be + 0.25 * al * al * al
    c5 = -0.75 * al * al * be
    c7 = 0.75 * al * be * be
    c9 = -0.25 * be * be * be
    u[...] = (c5 * v1f[...] + c7 * v3[...] + c9 * v5).astype(BF16)
    top = slice(0, 3 * w)
    cols[top, :] = mm(fb[top, :], u[...]) + (c1 * v1f[top, :] + c3 * v3[top, :])
    cols[bl(0), :] = cols[bl(0), :] + jnp.where(eye(w), 0.5, 0.0)
    after_x()
    top = slice(3 * w, n)
    cols[top, :] = mm(fb[top, :], u[...]) + (c1 * v1f[top, :] + c3 * v3[top, :])


def kernel(
    sizes, diag_hbm, x_hbm, y_hbm, lev_hbm, list_hbm, out_ref,
    din, xin, yin, lin, fin, in_sems,
    send1, rd1, rb1, send2, rd2, rc2, rf3,
    row0, v1, dk, sx, fb, v3, u, v1f, cols,
    send_sems, recv_sems,
):
    nx, ny = sizes
    w = din.shape[0]
    ix = lax.axis_index("space")
    iy = lax.axis_index("grp")
    has = [ix > 0, ix < nx - 1, iy > 0, iy < ny - 1]
    dev = [
        (jnp.maximum(ix - 1, 0), iy),
        (jnp.minimum(ix + 1, nx - 1), iy),
        (ix, jnp.maximum(iy - 1, 0)),
        (ix, jnp.minimum(iy + 1, ny - 1)),
    ]

    def bl(i):
        return slice(i * w, (i + 1) * w)

    barrier = pltpu.get_barrier_semaphore()
    for k in range(4):
        @pl.when(has[k])
        def _():
            pl.semaphore_signal(barrier, inc=1, device_id=dev[k], device_id_type=MESH)

    loads = [
        pltpu.make_async_copy(diag_hbm.at[0, 0], din, in_sems.at[0]),
        pltpu.make_async_copy(x_hbm.at[0, 0], xin, in_sems.at[1]),
        pltpu.make_async_copy(y_hbm.at[0, 0], yin, in_sems.at[2]),
        pltpu.make_async_copy(lev_hbm.at[0], lin, in_sems.at[3]),
        pltpu.make_async_copy(list_hbm.at[0], fin, in_sems.at[4]),
    ]
    for load in loads:
        load.start()
    for k in range(4):
        @pl.when(jnp.logical_not(has[k]))
        def _():
            zero = jnp.zeros((w, w), F32)
            rd1[k] = zero
            rd2[k] = zero
            rc2[k] = zero
            if k % 2 == 0:
                rb1[k // 2] = zero
            else:
                rf3[k // 2] = zero
    for load in loads:
        load.wait()
    one_eye = eye(w)
    flag_x = fin[0, 0].astype(F32) * (ix < nx - 1).astype(F32)
    flag_y = fin[0, 1].astype(F32) * (iy < ny - 1).astype(F32)
    raw = din[...]
    onsite = 0.5 * (raw + raw.T) + jnp.where(one_eye, jnp.broadcast_to(lin[...], (w, w)), 0.0)
    send1[0] = onsite
    send1[1] = xin[...] * flag_x
    send1[2] = yin[...] * flag_y

    count = sum(h.astype(jnp.int32) for h in has)
    pl.semaphore_wait(barrier, count)

    def transfer(src, dst, index_send, index_recv, k):
        return pltpu.make_async_remote_copy(
            src_ref=src, dst_ref=dst, send_sem=send_sems.at[index_send],
            recv_sem=recv_sems.at[index_recv], device_id=dev[k], device_id_type=MESH,
        )

    def diag1(k):
        return transfer(send1.at[0], rd1.at[k ^ 1], k, k ^ 1, k)

    def coup1(k):
        return transfer(send1.at[1 + k // 2], rb1.at[k // 2], 4 + k // 2, 4 + k // 2, k)

    def diag2(k):
        return transfer(send2, rd2.at[k ^ 1], 6 + k, 6 + (k ^ 1), k)

    def coup2(k):
        return transfer(cols1.at[bl(1 + k), :], rc2.at[k ^ 1], 10 + k, 10 + (k ^ 1), k)

    def coup3(k):
        return transfer(cols2.at[bl(1 + k), :], rf3.at[k // 2], 14 + k // 2, 14 + k // 2, k)

    cols1, cols2 = cols.at[0], cols.at[1]

    order = (1, 0, 3, 2)
    for k in order:
        @pl.when(has[k])
        def _():
            if k % 2:
                coup1(k).start()
            diag1(k).start()

    row0[:, bl(0)] = onsite.astype(BF16)
    v1[bl(0), :] = onsite.astype(BF16)
    v1f[bl(0), :] = onsite
    for axis in range(2):
        coup = send1[1 + axis]
        coup_t = coup.T
        row0[:, bl(2 + 2 * axis)] = coup.astype(BF16)
        v1[bl(2 + 2 * axis), :] = coup_t.astype(BF16)
        v1f[bl(2 + 2 * axis), :] = coup_t
    def arrived1(slots):
        for k in (2, 3, 1, 0):
            @pl.when(has[k])
            def _():
                if k % 2 == 0:
                    coup1(k ^ 1).wait_recv()
                diag1(k ^ 1).wait_recv()
            dk[k] = rd1[k].astype(BF16)
            if k % 2 == 0:
                coup = rb1[k // 2]
                row0[:, bl(1 + k)] = coup.T.astype(BF16)
                v1[bl(1 + k), :] = coup.astype(BF16)
                v1f[bl(1 + k), :] = coup
            yield k

    onsite_two = []

    def send_x2():
        for k in (1, 0):
            @pl.when(has[k])
            def _():
                coup2(k).start()
        c0 = cols1[bl(0), :]
        two = v1f[bl(0), :] + hubbard * (0.5 * (c0 + c0.T) - jnp.where(one_eye, 0.5, 0.0))
        send2[...] = two
        onsite_two.append(two)
        for k in order:
            @pl.when(has[k])
            def _():
                diag2(k).start()

    density_columns(w, row0, v1, dk, sx, fb, v3, u, v1f, cols1, send_x2, arrived1)

    for k in (3, 2):
        @pl.when(has[k])
        def _():
            coup2(k).start()
    two = onsite_two[0]
    row0[:, bl(0)] = two.astype(BF16)
    v1[bl(0), :] = two.astype(BF16)
    v1f[bl(0), :] = two
    for k in range(4):
        v1f[bl(1 + k), :] = v1f[bl(1 + k), :] + 0.5 * hubbard * cols1[bl(1 + k), :]

    def arrived2(slots):
        for k in (2, 3, 1, 0):
            @pl.when(has[k])
            def _():
                coup2(k ^ 1).wait_recv()
                diag2(k ^ 1).wait_recv()
            dk[k] = rd2[k].astype(BF16)
            bk = v1f[bl(1 + k), :] + 0.5 * hubbard * rc2[k].T
            v1f[bl(1 + k), :] = bk
            v1[bl(1 + k), :] = bk.astype(BF16)
            row0[:, bl(1 + k)] = bk.T.astype(BF16)
            yield k

    def send_x3():
        @pl.when(has[0])
        def _():
            coup3(0).start()

    density_columns(w, row0, v1, dk, sx, fb, v3, u, v1f, cols2, send_x3, arrived2)

    @pl.when(has[2])
    def _():
        coup3(2).start()
    c0 = cols2[bl(0), :]
    out_ref[0] = 0.5 * (c0 + c0.T)
    half_x = 0.5 * cols2[bl(2), :].T
    half_y = 0.5 * cols2[bl(4), :].T
    for k in (3, 1):
        @pl.when(has[k])
        def _():
            coup3(k ^ 1).wait_recv()
    out_ref[1] = half_x + 0.5 * rf3[0]
    out_ref[2] = half_y + 0.5 * rf3[1]
    for k in range(4):
        @pl.when(has[k])
        def _():
            if k % 2:
                coup1(k).wait_send()
            else:
                coup3(k).wait_send()
            diag1(k).wait_send()
            coup2(k).wait_send()
            diag2(k).wait_send()


def write_out(in_ref, od_ref, ox_ref, oy_ref, sems):
    copies = [
        pltpu.make_async_copy(in_ref.at[i], ref.at[0, 0], sems.at[i])
        for i, ref in enumerate((od_ref, ox_ref, oy_ref))
    ]
    for copy in copies:
        copy.start()
    for copy in copies:
        copy.wait()


def per_device(diag_blocks, x_coupling, y_coupling, levels, listed):
    w = diag_blocks.shape[-1]
    n = 5 * w
    sizes = (lax.axis_size("space"), lax.axis_size("grp"))
    block = jax.ShapeDtypeStruct((1, 1, w, w), F32)
    any_spec = pl.BlockSpec(memory_space=pl.ANY)
    vmem_spec = pl.BlockSpec(memory_space=pltpu.VMEM)
    results = pl.pallas_call(
        functools.partial(kernel, sizes),
        out_shape=pltpu.VMEM((3, w, w), F32),
        in_specs=[any_spec] * 5,
        out_specs=vmem_spec,
        scratch_shapes=[
            pltpu.VMEM((w, w), F32),
            pltpu.VMEM((w, w), F32),
            pltpu.VMEM((w, w), F32),
            pltpu.VMEM((1, w), F32),
            pltpu.SMEM((1, 2), jnp.int32),
            pltpu.SemaphoreType.DMA((5,)),
            pltpu.VMEM((3, w, w), F32),
            pltpu.VMEM((4, w, w), F32),
            pltpu.VMEM((2, w, w), F32),
            pltpu.VMEM((w, w), F32),
            pltpu.VMEM((4, w, w), F32),
            pltpu.VMEM((4, w, w), F32),
            pltpu.VMEM((2, w, w), F32),
            pltpu.VMEM((w, n), BF16),
            pltpu.VMEM((n, w), BF16),
            pltpu.VMEM((4, w, w), BF16),
            pltpu.VMEM((n, n + w), BF16),
            pltpu.VMEM((n, n), BF16),
            pltpu.VMEM((n, w), F32),
            pltpu.VMEM((n, w), BF16),
            pltpu.VMEM((n, w), F32),
            pltpu.VMEM((2, n, w), F32),
            pltpu.SemaphoreType.DMA((16,)),
            pltpu.SemaphoreType.DMA((16,)),
        ],
        compiler_params=pltpu.CompilerParams(collective_id=0, has_side_effects=True),
    )(diag_blocks, x_coupling, y_coupling, levels, listed)
    return pl.pallas_call(
        write_out,
        out_shape=(block, block, block),
        in_specs=[vmem_spec],
        out_specs=(any_spec,) * 3,
        scratch_shapes=[pltpu.SemaphoreType.DMA((3,))],
    )(pltpu.with_memory_space_constraint(results, pltpu.VMEM))


def solution(mesh):
    blocks = P("space", "grp", None, None)
    rows = P("space", "grp", None)
    return jax.shard_map(
        per_device,
        mesh=mesh,
        in_specs=(blocks, blocks, blocks, rows, rows),
        out_specs=(blocks, blocks, blocks),
        check_vma=False,
    )
```

```python
import functools

import jax
import jax.numpy as jnp
from jax import lax
from jax.experimental import pallas as pl
from jax.experimental.pallas import tpu as pltpu
from jax.sharding import PartitionSpec as P

hubbard = 1.0
MESH = pl.DeviceIdType.MESH
F32 = jnp.float32
BF16 = jnp.bfloat16


def mm(a, b):
    return jnp.dot(a, b, preferred_element_type=F32)


def eye(w):
    return lax.broadcasted_iota(jnp.int32, (w, w), 0) == lax.broadcasted_iota(jnp.int32, (w, w), 1)


def density_columns(w, row0, v1, dk, sx, fb, v3, u, v1f, cols, after_x, arrived):
    n = 5 * w

    def bl(i):
        return slice(i * w, (i + 1) * w)

    d0 = row0[:, bl(0)]
    for k in arrived(range(4)):
        top = jnp.concatenate([d0, row0[:, bl(1 + k)]], axis=1)
        low = jnp.concatenate([v1[bl(1 + k), :], dk[k]], axis=1)
        pair = jnp.concatenate([top, low], axis=0)
        part = mm(pair, pair).astype(BF16)
        sx[bl(0), bl(1 + k)] = part[:w, w:]
        sx[bl(1 + k), bl(0)] = part[w:, :w]
        sx[bl(1 + k), bl(1 + k)] = part[w:, w:]
    sx[bl(0), bl(0)] = mm(row0[...], v1[...]).astype(BF16)
    for half in range(2):
        t = mm(v1[w:, :], row0[:, w * (1 + 2 * half) : w * (3 + 2 * half)])
        for l in (0, 1):
            k = 2 * half + l
            for r in range(4):
                if r != k:
                    sx[bl(1 + r), bl(1 + k)] = t[bl(r), bl(l)].astype(BF16)
    first = mm(row0[...], sx[:, bl(0)])
    v3[bl(0), :] = first
    sx[bl(0), n:] = first.astype(BF16)
    for k in range(4):
        low = jnp.concatenate([v1[bl(1 + k), :], dk[k]], axis=1)
        vec = jnp.concatenate([sx[bl(0), bl(0)], sx[bl(1 + k), bl(0)]], axis=0)
        first = mm(low, vec)
        v3[bl(1 + k), :] = first
        sx[bl(1 + k), n:] = first.astype(BF16)
    total = jnp.zeros((1, 2 * w), F32)
    for c in range(2):
        f = mm(sx[:, :n], sx[:, 2 * w * c : 2 * w * (c + 1)])
        fb[:, 2 * w * c : 2 * w * (c + 1)] = f.astype(BF16)
        total = total + jnp.sum(f * f, axis=0, keepdims=True)
    f = mm(sx[:, :n], sx[:, 4 * w :])
    v5 = f[:, w:]
    f = f[:, :w]
    fb[:, 4 * w :] = f.astype(BF16)
    total = total[:, :w] + total[:, w:] + jnp.sum(f * f, axis=0, keepdims=True)
    squares = jnp.sum(total, axis=1, keepdims=True)
    scale_two = jnp.sqrt(jnp.sqrt(squares + 1e-06))
    scale_one = jnp.sqrt(scale_two)
    al = 1.5 / scale_one
    be = 0.5 / (scale_one * scale_two)
    c1 = -0.75 * al
    c3 = 0.75 * be + 0.25 * al * al * al
    c5 = -0.75 * al * al * be
    c7 = 0.75 * al * be * be
    c9 = -0.25 * be * be * be
    u[...] = (c5 * v1f[...] + c7 * v3[...] + c9 * v5).astype(BF16)
    top = slice(0, 3 * w)
    cols[top, :] = mm(fb[top, :], u[...]) + (c1 * v1f[top, :] + c3 * v3[top, :])
    cols[bl(0), :] = cols[bl(0), :] + jnp.where(eye(w), 0.5, 0.0)
    after_x()
    top = slice(3 * w, n)
    cols[top, :] = mm(fb[top, :], u[...]) + (c1 * v1f[top, :] + c3 * v3[top, :])


def kernel(
    sizes, diag_hbm, x_hbm, y_hbm, lev_hbm, list_hbm, out_ref,
    din, xin, yin, lin, fin, in_sems,
    send1, rd1, rb1, send2, rd2, rc2, rf3,
    row0, v1, dk, sx, fb, v3, u, v1f, cols,
    send_sems, recv_sems,
):
    nx, ny = sizes
    w = din.shape[0]
    ix = lax.axis_index("space")
    iy = lax.axis_index("grp")
    has = [ix > 0, ix < nx - 1, iy > 0, iy < ny - 1]
    dev = [
        (jnp.maximum(ix - 1, 0), iy),
        (jnp.minimum(ix + 1, nx - 1), iy),
        (ix, jnp.maximum(iy - 1, 0)),
        (ix, jnp.minimum(iy + 1, ny - 1)),
    ]

    def bl(i):
        return slice(i * w, (i + 1) * w)

    barrier = pltpu.get_barrier_semaphore()
    for k in range(4):
        @pl.when(has[k])
        def _():
            pl.semaphore_signal(barrier, inc=1, device_id=dev[k], device_id_type=MESH)

    loads = [
        pltpu.make_async_copy(diag_hbm.at[0, 0], din, in_sems.at[0]),
        pltpu.make_async_copy(x_hbm.at[0, 0], xin, in_sems.at[1]),
        pltpu.make_async_copy(y_hbm.at[0, 0], yin, in_sems.at[2]),
        pltpu.make_async_copy(lev_hbm.at[0], lin, in_sems.at[3]),
        pltpu.make_async_copy(list_hbm.at[0], fin, in_sems.at[4]),
    ]
    for load in loads:
        load.start()
    for k in range(4):
        @pl.when(jnp.logical_not(has[k]))
        def _():
            zero = jnp.zeros((w, w), F32)
            rd1[k] = zero
            rd2[k] = zero
            rc2[k] = zero
            if k % 2 == 0:
                rb1[k // 2] = zero
            else:
                rf3[k // 2] = zero
    for load in loads:
        load.wait()
    one_eye = eye(w)
    flag_x = fin[0, 0].astype(F32) * (ix < nx - 1).astype(F32)
    flag_y = fin[0, 1].astype(F32) * (iy < ny - 1).astype(F32)
    raw = din[...]
    onsite = 0.5 * (raw + raw.T) + jnp.where(one_eye, jnp.broadcast_to(lin[...], (w, w)), 0.0)
    send1[0] = onsite
    send1[1] = xin[...] * flag_x
    send1[2] = yin[...] * flag_y

    count = sum(h.astype(jnp.int32) for h in has)
    pl.semaphore_wait(barrier, count)

    def transfer(src, dst, index_send, index_recv, k):
        return pltpu.make_async_remote_copy(
            src_ref=src, dst_ref=dst, send_sem=send_sems.at[index_send],
            recv_sem=recv_sems.at[index_recv], device_id=dev[k], device_id_type=MESH,
        )

    def diag1(k):
        return transfer(send1.at[0], rd1.at[k ^ 1], k, k ^ 1, k)

    def coup1(k):
        return transfer(send1.at[1 + k // 2], rb1.at[k // 2], 4 + k // 2, 4 + k // 2, k)

    def diag2(k):
        return transfer(send2, rd2.at[k ^ 1], 6 + k, 6 + (k ^ 1), k)

    def coup2(k):
        return transfer(cols1.at[bl(1 + k), :], rc2.at[k ^ 1], 10 + k, 10 + (k ^ 1), k)

    def coup3(k):
        return transfer(cols2.at[bl(1 + k), :], rf3.at[k // 2], 14 + k // 2, 14 + k // 2, k)

    cols1, cols2 = cols.at[0], cols.at[1]

    order = (1, 0, 3, 2)
    for k in order:
        @pl.when(has[k])
        def _():
            if k % 2:
                coup1(k).start()
            diag1(k).start()

    row0[:, bl(0)] = onsite.astype(BF16)
    v1[bl(0), :] = onsite.astype(BF16)
    v1f[bl(0), :] = onsite
    for axis in range(2):
        coup = send1[1 + axis]
        coup_t = coup.T
        row0[:, bl(2 + 2 * axis)] = coup.astype(BF16)
        v1[bl(2 + 2 * axis), :] = coup_t.astype(BF16)
        v1f[bl(2 + 2 * axis), :] = coup_t
    def arrived1(slots):
        for group in ((2, 3), (1, 0)):
            for k in group:
                @pl.when(has[k])
                def _():
                    if k % 2 == 0:
                        coup1(k ^ 1).wait_recv()
                    diag1(k ^ 1).wait_recv()
            for k in group:
                dk[k] = rd1[k].astype(BF16)
                if k % 2 == 0:
                    coup = rb1[k // 2]
                    row0[:, bl(1 + k)] = coup.T.astype(BF16)
                    v1[bl(1 + k), :] = coup.astype(BF16)
                    v1f[bl(1 + k), :] = coup
            yield from group

    onsite_two = []

    def send_x2():
        for k in (1, 0):
            @pl.when(has[k])
            def _():
                coup2(k).start()
        c0 = cols1[bl(0), :]
        two = v1f[bl(0), :] + hubbard * (0.5 * (c0 + c0.T) - jnp.where(one_eye, 0.5, 0.0))
        send2[...] = two
        onsite_two.append(two)
        for k in order:
            @pl.when(has[k])
            def _():
                diag2(k).start()

    density_columns(w, row0, v1, dk, sx, fb, v3, u, v1f, cols1, send_x2, arrived1)

    for k in (3, 2):
        @pl.when(has[k])
        def _():
            coup2(k).start()
    two = onsite_two[0]
    row0[:, bl(0)] = two.astype(BF16)
    v1[bl(0), :] = two.astype(BF16)
    v1f[bl(0), :] = two
    for k in range(4):
        v1f[bl(1 + k), :] = v1f[bl(1 + k), :] + 0.5 * hubbard * cols1[bl(1 + k), :]

    def arrived2(slots):
        for group in ((2, 3), (1, 0)):
            for k in group:
                @pl.when(has[k])
                def _():
                    coup2(k ^ 1).wait_recv()
                    diag2(k ^ 1).wait_recv()
            for k in group:
                dk[k] = rd2[k].astype(BF16)
                bk = v1f[bl(1 + k), :] + 0.5 * hubbard * rc2[k].T
                v1f[bl(1 + k), :] = bk
                v1[bl(1 + k), :] = bk.astype(BF16)
                row0[:, bl(1 + k)] = bk.T.astype(BF16)
            yield from group

    def send_x3():
        @pl.when(has[0])
        def _():
            coup3(0).start()

    density_columns(w, row0, v1, dk, sx, fb, v3, u, v1f, cols2, send_x3, arrived2)

    @pl.when(has[2])
    def _():
        coup3(2).start()
    c0 = cols2[bl(0), :]
    out_ref[0] = 0.5 * (c0 + c0.T)
    half_x = 0.5 * cols2[bl(2), :].T
    half_y = 0.5 * cols2[bl(4), :].T
    for k in (3, 1):
        @pl.when(has[k])
        def _():
            coup3(k ^ 1).wait_recv()
    out_ref[1] = half_x + 0.5 * rf3[0]
    out_ref[2] = half_y + 0.5 * rf3[1]
    for k in range(4):
        @pl.when(has[k])
        def _():
            if k % 2:
                coup1(k).wait_send()
            else:
                coup3(k).wait_send()
            diag1(k).wait_send()
            coup2(k).wait_send()
            diag2(k).wait_send()


def write_out(in_ref, od_ref, ox_ref, oy_ref, sems):
    copies = [
        pltpu.make_async_copy(in_ref.at[i], ref.at[0, 0], sems.at[i])
        for i, ref in enumerate((od_ref, ox_ref, oy_ref))
    ]
    for copy in copies:
        copy.start()
    for copy in copies:
        copy.wait()


def per_device(diag_blocks, x_coupling, y_coupling, levels, listed):
    w = diag_blocks.shape[-1]
    n = 5 * w
    sizes = (lax.axis_size("space"), lax.axis_size("grp"))
    block = jax.ShapeDtypeStruct((1, 1, w, w), F32)
    any_spec = pl.BlockSpec(memory_space=pl.ANY)
    vmem_spec = pl.BlockSpec(memory_space=pltpu.VMEM)
    results = pl.pallas_call(
        functools.partial(kernel, sizes),
        out_shape=pltpu.VMEM((3, w, w), F32),
        in_specs=[any_spec] * 5,
        out_specs=vmem_spec,
        scratch_shapes=[
            pltpu.VMEM((w, w), F32),
            pltpu.VMEM((w, w), F32),
            pltpu.VMEM((w, w), F32),
            pltpu.VMEM((1, w), F32),
            pltpu.SMEM((1, 2), jnp.int32),
            pltpu.SemaphoreType.DMA((5,)),
            pltpu.VMEM((3, w, w), F32),
            pltpu.VMEM((4, w, w), F32),
            pltpu.VMEM((2, w, w), F32),
            pltpu.VMEM((w, w), F32),
            pltpu.VMEM((4, w, w), F32),
            pltpu.VMEM((4, w, w), F32),
            pltpu.VMEM((2, w, w), F32),
            pltpu.VMEM((w, n), BF16),
            pltpu.VMEM((n, w), BF16),
            pltpu.VMEM((4, w, w), BF16),
            pltpu.VMEM((n, n + w), BF16),
            pltpu.VMEM((n, n), BF16),
            pltpu.VMEM((n, w), F32),
            pltpu.VMEM((n, w), BF16),
            pltpu.VMEM((n, w), F32),
            pltpu.VMEM((2, n, w), F32),
            pltpu.SemaphoreType.DMA((16,)),
            pltpu.SemaphoreType.DMA((16,)),
        ],
        compiler_params=pltpu.CompilerParams(collective_id=0, has_side_effects=True),
    )(diag_blocks, x_coupling, y_coupling, levels, listed)
    return pl.pallas_call(
        write_out,
        out_shape=(block, block, block),
        in_specs=[vmem_spec],
        out_specs=(any_spec,) * 3,
        scratch_shapes=[pltpu.SemaphoreType.DMA((3,))],
    )(pltpu.with_memory_space_constraint(results, pltpu.VMEM))


def solution(mesh):
    blocks = P("space", "grp", None, None)
    rows = P("space", "grp", None)
    return jax.shard_map(
        per_device,
        mesh=mesh,
        in_specs=(blocks, blocks, blocks, rows, rows),
        out_specs=(blocks, blocks, blocks),
        check_vma=False,
    )
```

```python
import functools

import jax
import jax.numpy as jnp
from jax import lax
from jax.experimental import pallas as pl
from jax.experimental.pallas import tpu as pltpu
from jax.sharding import PartitionSpec as P

hubbard = 1.0
MESH = pl.DeviceIdType.MESH
F32 = jnp.float32
BF16 = jnp.bfloat16


def mm(a, b):
    return jnp.dot(a, b, preferred_element_type=F32)


def eye(w):
    return lax.broadcasted_iota(jnp.int32, (w, w), 0) == lax.broadcasted_iota(jnp.int32, (w, w), 1)


def density_columns(w, row0, v1, dk, sx, fb, v3, u, v1f, cols, after_x, arrived):
    n = 5 * w

    def bl(i):
        return slice(i * w, (i + 1) * w)

    d0 = row0[:, bl(0)]
    for k in arrived(range(4)):
        top = jnp.concatenate([d0, row0[:, bl(1 + k)]], axis=1)
        low = jnp.concatenate([v1[bl(1 + k), :], dk[k]], axis=1)
        pair = jnp.concatenate([top, low], axis=0)
        part = mm(pair, pair).astype(BF16)
        sx[bl(0), bl(1 + k)] = part[:w, w:]
        sx[bl(1 + k), bl(0)] = part[w:, :w]
        sx[bl(1 + k), bl(1 + k)] = part[w:, w:]
    sx[bl(0), bl(0)] = mm(row0[...], v1[...]).astype(BF16)
    for half in range(2):
        t = mm(v1[w:, :], row0[:, w * (1 + 2 * half) : w * (3 + 2 * half)])
        for l in (0, 1):
            k = 2 * half + l
            for r in range(4):
                if r != k:
                    sx[bl(1 + r), bl(1 + k)] = t[bl(r), bl(l)].astype(BF16)
    first = mm(row0[...], sx[:, bl(0)])
    v3[bl(0), :] = first
    sx[bl(0), n:] = first.astype(BF16)
    for k in range(4):
        low = jnp.concatenate([v1[bl(1 + k), :], dk[k]], axis=1)
        vec = jnp.concatenate([sx[bl(0), bl(0)], sx[bl(1 + k), bl(0)]], axis=0)
        first = mm(low, vec)
        v3[bl(1 + k), :] = first
        sx[bl(1 + k), n:] = first.astype(BF16)
    total = jnp.zeros((1, 2 * w), F32)
    for c in range(2):
        f = mm(sx[:, :n], sx[:, 2 * w * c : 2 * w * (c + 1)])
        fb[:, 2 * w * c : 2 * w * (c + 1)] = f.astype(BF16)
        total = total + jnp.sum(f * f, axis=0, keepdims=True)
    f = mm(sx[:, :n], sx[:, 4 * w :])
    v5 = f[:, w:]
    f = f[:, :w]
    fb[:, 4 * w :] = f.astype(BF16)
    total = total[:, :w] + total[:, w:] + jnp.sum(f * f, axis=0, keepdims=True)
    squares = jnp.sum(total, axis=1, keepdims=True)
    scale_two = jnp.sqrt(jnp.sqrt(squares + 1e-06))
    scale_one = jnp.sqrt(scale_two)
    al = 1.5 / scale_one
    be = 0.5 / (scale_one * scale_two)
    c1 = -0.75 * al
    c3 = 0.75 * be + 0.25 * al * al * al
    c5 = -0.75 * al * al * be
    c7 = 0.75 * al * be * be
    c9 = -0.25 * be * be * be
    u[...] = (c5 * v1f[...] + c7 * v3[...] + c9 * v5).astype(BF16)
    top = slice(0, 3 * w)
    cols[top, :] = mm(fb[top, :], u[...]) + (c1 * v1f[top, :] + c3 * v3[top, :])
    cols[bl(0), :] = cols[bl(0), :] + jnp.where(eye(w), 0.5, 0.0)
    after_x()
    top = slice(3 * w, n)
    cols[top, :] = mm(fb[top, :], u[...]) + (c1 * v1f[top, :] + c3 * v3[top, :])


def kernel(
    sizes, diag_hbm, x_hbm, y_hbm, lev_hbm, list_hbm, out_ref,
    din, xin, yin, lin, fin, in_sems,
    send1, rd1, rb1, send2, rd2, rc2, rf3,
    row0, v1, dk, sx, fb, v3, u, v1f, cols, rowf,
    send_sems, recv_sems,
):
    nx, ny = sizes
    w = din.shape[0]
    ix = lax.axis_index("space")
    iy = lax.axis_index("grp")
    has = [ix > 0, ix < nx - 1, iy > 0, iy < ny - 1]
    dev = [
        (jnp.maximum(ix - 1, 0), iy),
        (jnp.minimum(ix + 1, nx - 1), iy),
        (ix, jnp.maximum(iy - 1, 0)),
        (ix, jnp.minimum(iy + 1, ny - 1)),
    ]

    def bl(i):
        return slice(i * w, (i + 1) * w)

    barrier = pltpu.get_barrier_semaphore()
    for k in range(4):
        @pl.when(has[k])
        def _():
            pl.semaphore_signal(barrier, inc=1, device_id=dev[k], device_id_type=MESH)

    loads = [
        pltpu.make_async_copy(diag_hbm.at[0, 0], din, in_sems.at[0]),
        pltpu.make_async_copy(x_hbm.at[0, 0], xin, in_sems.at[1]),
        pltpu.make_async_copy(y_hbm.at[0, 0], yin, in_sems.at[2]),
        pltpu.make_async_copy(lev_hbm.at[0], lin, in_sems.at[3]),
        pltpu.make_async_copy(list_hbm.at[0], fin, in_sems.at[4]),
    ]
    for load in loads:
        load.start()
    for k in range(4):
        @pl.when(jnp.logical_not(has[k]))
        def _():
            zero = jnp.zeros((w, w), F32)
            rd1[k] = zero
            rd2[k] = zero
            rc2[k] = zero
            if k % 2 == 0:
                rb1[k // 2] = zero
            else:
                rf3[k // 2] = zero
    for load in loads:
        load.wait()
    one_eye = eye(w)
    flag_x = fin[0, 0].astype(F32) * (ix < nx - 1).astype(F32)
    flag_y = fin[0, 1].astype(F32) * (iy < ny - 1).astype(F32)
    raw = din[...]
    onsite = 0.5 * (raw + raw.T) + jnp.where(one_eye, jnp.broadcast_to(lin[...], (w, w)), 0.0)
    send1[0] = onsite
    send1[1] = xin[...] * flag_x
    send1[2] = yin[...] * flag_y

    count = sum(h.astype(jnp.int32) for h in has)
    pl.semaphore_wait(barrier, count)

    def transfer(src, dst, index_send, index_recv, k):
        return pltpu.make_async_remote_copy(
            src_ref=src, dst_ref=dst, send_sem=send_sems.at[index_send],
            recv_sem=recv_sems.at[index_recv], device_id=dev[k], device_id_type=MESH,
        )

    def diag1(k):
        return transfer(send1.at[0], rd1.at[k ^ 1], k, k ^ 1, k)

    def coup1(k):
        return transfer(send1.at[1 + k // 2], rb1.at[k // 2], 4 + k // 2, 4 + k // 2, k)

    def diag2(k):
        return transfer(send2, rd2.at[k ^ 1], 6 + k, 6 + (k ^ 1), k)

    def coup2(k):
        return transfer(cols1.at[bl(1 + k), :], rc2.at[k ^ 1], 10 + k, 10 + (k ^ 1), k)

    def coup3(k):
        return transfer(cols2.at[bl(1 + k), :], rf3.at[k // 2], 14 + k // 2, 14 + k // 2, k)

    cols1, cols2 = cols.at[0], cols.at[1]

    order = (1, 0, 3, 2)
    for k in order:
        @pl.when(has[k])
        def _():
            if k % 2:
                coup1(k).start()
            diag1(k).start()

    row0[:, bl(0)] = onsite.astype(BF16)
    v1[bl(0), :] = onsite.astype(BF16)
    v1f[bl(0), :] = onsite
    for axis in range(2):
        coup = send1[1 + axis]
        coup_t = coup.T
        row0[:, bl(2 + 2 * axis)] = coup.astype(BF16)
        v1[bl(2 + 2 * axis), :] = coup_t.astype(BF16)
        v1f[bl(2 + 2 * axis), :] = coup_t
    def arrived1(slots):
        for group in ((2, 3), (1, 0)):
            for k in group:
                @pl.when(has[k])
                def _():
                    if k % 2 == 0:
                        coup1(k ^ 1).wait_recv()
                    diag1(k ^ 1).wait_recv()
            for k in group:
                dk[k] = rd1[k].astype(BF16)
                if k % 2 == 0:
                    coup = rb1[k // 2]
                    row0[:, bl(1 + k)] = coup.T.astype(BF16)
                    v1[bl(1 + k), :] = coup.astype(BF16)
                    v1f[bl(1 + k), :] = coup
            yield from group

    onsite_two = []

    def send_x2():
        for k in (1, 0):
            @pl.when(has[k])
            def _():
                coup2(k).start()
        c0 = cols1[bl(0), :]
        two = v1f[bl(0), :] + hubbard * (0.5 * (c0 + c0.T) - jnp.where(one_eye, 0.5, 0.0))
        send2[...] = two
        onsite_two.append(two)
        for k in order:
            @pl.when(has[k])
            def _():
                diag2(k).start()

    density_columns(w, row0, v1, dk, sx, fb, v3, u, v1f, cols1, send_x2, arrived1)

    for k in (3, 2):
        @pl.when(has[k])
        def _():
            coup2(k).start()
    two = onsite_two[0]
    row0[:, bl(0)] = two.astype(BF16)
    v1[bl(0), :] = two.astype(BF16)
    v1f[bl(0), :] = two
    for k in range(4):
        rowf[k] = (v1f[bl(1 + k), :] + 0.5 * hubbard * cols1[bl(1 + k), :]).T

    def arrived2(slots):
        for group in ((2, 3), (1, 0)):
            for k in group:
                @pl.when(has[k])
                def _():
                    coup2(k ^ 1).wait_recv()
                    diag2(k ^ 1).wait_recv()
            for k in group:
                dk[k] = rd2[k].astype(BF16)
                btk = rowf[k] + 0.5 * hubbard * rc2[k]
                row0[:, bl(1 + k)] = btk.astype(BF16)
                bk = btk.T
                v1f[bl(1 + k), :] = bk
                v1[bl(1 + k), :] = bk.astype(BF16)
            yield from group

    def send_x3():
        @pl.when(has[0])
        def _():
            coup3(0).start()

    density_columns(w, row0, v1, dk, sx, fb, v3, u, v1f, cols2, send_x3, arrived2)

    @pl.when(has[2])
    def _():
        coup3(2).start()
    c0 = cols2[bl(0), :]
    out_ref[0] = 0.5 * (c0 + c0.T)
    half_x = 0.5 * cols2[bl(2), :].T
    half_y = 0.5 * cols2[bl(4), :].T
    for k in (3, 1):
        @pl.when(has[k])
        def _():
            coup3(k ^ 1).wait_recv()
    out_ref[1] = half_x + 0.5 * rf3[0]
    out_ref[2] = half_y + 0.5 * rf3[1]
    for k in range(4):
        @pl.when(has[k])
        def _():
            if k % 2:
                coup1(k).wait_send()
            else:
                coup3(k).wait_send()
            diag1(k).wait_send()
            coup2(k).wait_send()
            diag2(k).wait_send()


def write_out(in_ref, od_ref, ox_ref, oy_ref, sems):
    copies = [
        pltpu.make_async_copy(in_ref.at[i], ref.at[0, 0], sems.at[i])
        for i, ref in enumerate((od_ref, ox_ref, oy_ref))
    ]
    for copy in copies:
        copy.start()
    for copy in copies:
        copy.wait()


def per_device(diag_blocks, x_coupling, y_coupling, levels, listed):
    w = diag_blocks.shape[-1]
    n = 5 * w
    sizes = (lax.axis_size("space"), lax.axis_size("grp"))
    block = jax.ShapeDtypeStruct((1, 1, w, w), F32)
    any_spec = pl.BlockSpec(memory_space=pl.ANY)
    vmem_spec = pl.BlockSpec(memory_space=pltpu.VMEM)
    results = pl.pallas_call(
        functools.partial(kernel, sizes),
        out_shape=pltpu.VMEM((3, w, w), F32),
        in_specs=[any_spec] * 5,
        out_specs=vmem_spec,
        scratch_shapes=[
            pltpu.VMEM((w, w), F32),
            pltpu.VMEM((w, w), F32),
            pltpu.VMEM((w, w), F32),
            pltpu.VMEM((1, w), F32),
            pltpu.SMEM((1, 2), jnp.int32),
            pltpu.SemaphoreType.DMA((5,)),
            pltpu.VMEM((3, w, w), F32),
            pltpu.VMEM((4, w, w), F32),
            pltpu.VMEM((2, w, w), F32),
            pltpu.VMEM((w, w), F32),
            pltpu.VMEM((4, w, w), F32),
            pltpu.VMEM((4, w, w), F32),
            pltpu.VMEM((2, w, w), F32),
            pltpu.VMEM((w, n), BF16),
            pltpu.VMEM((n, w), BF16),
            pltpu.VMEM((4, w, w), BF16),
            pltpu.VMEM((n, n + w), BF16),
            pltpu.VMEM((n, n), BF16),
            pltpu.VMEM((n, w), F32),
            pltpu.VMEM((n, w), BF16),
            pltpu.VMEM((n, w), F32),
            pltpu.VMEM((2, n, w), F32),
            pltpu.VMEM((4, w, w), F32),
            pltpu.SemaphoreType.DMA((16,)),
            pltpu.SemaphoreType.DMA((16,)),
        ],
        compiler_params=pltpu.CompilerParams(collective_id=0, has_side_effects=True),
    )(diag_blocks, x_coupling, y_coupling, levels, listed)
    return pl.pallas_call(
        write_out,
        out_shape=(block, block, block),
        in_specs=[vmem_spec],
        out_specs=(any_spec,) * 3,
        scratch_shapes=[pltpu.SemaphoreType.DMA((3,))],
    )(pltpu.with_memory_space_constraint(results, pltpu.VMEM))


def solution(mesh):
    blocks = P("space", "grp", None, None)
    rows = P("space", "grp", None)
    return jax.shard_map(
        per_device,
        mesh=mesh,
        in_specs=(blocks, blocks, blocks, rows, rows),
        out_specs=(blocks, blocks, blocks),
        check_vma=False,
    )
```
